1024 devices in a mesh: blk: 16 (over x, z_hi), grp: 64 (over z_lo, y, core).
Axes of the slice: x: 4, y: 8, z: 16 (z_hi: 4, z_lo: 4; z = z_hi * 4 + z_lo), core: 2. Of those that a mesh axis runs over, the one named last changes fastest.
Arguments:
- amplitudes: bfloat16 [8192, 49152], P(('blk', 'grp')), may hold values from -6 to 6
- integrals: bfloat16 [49152, 2048], P('grp', 'blk'), may hold values from -0.0390625 to 0.0390625
- tile_mask: int32 [1024, 384], P(('blk', 'grp')), may hold values from 0 to 1, as said below
- tile_size: int32 [384], replicated, may hold values from 64 to 128, as said below
Outputs:
- ladder: bfloat16 [8192, 2048], P(('blk', 'grp'))
The draws below stay inside these ranges and needn't reach their ends.
Inputs may be any that keep to these rules, and one draw needn't show every extreme that they name: `tile_mask`: mask entries are 0 or 1; domains differ in how many of their tiles are live. `tile_size`: one tile is full and one is half full.
All inputs are finite; a program needn't handle non-finite values.
Results may differ from the reference program's by a relative error of at most 0.001.
Values may be sent and summed in bfloat16 or wider, within the bound.
A program may use at most 32 MiB of HBM per device.

```python
import math
import jax
import jax.numpy as jnp
from jax import lax

TILE = 128
ROWS_DEV = 8
DOMAINS = 1024
ROWS = 8192
NTILES = 384
NCD = 49152
NAB = 2048


def draw_tile_mask(key, part):
    level_key = jax.random.fold_in(key, 11)
    entry_key = jax.random.fold_in(key, 23)
    level = jax.random.randint(level_key, (DOMAINS, 1), 3, 9)
    entries = jax.random.randint(entry_key, (DOMAINS, NTILES), 0, 8)
    mask_values = (entries < level).astype(jnp.int32)
    mask_values = mask_values.at[0, 0].set(1)
    mask_values = mask_values.at[0, 1].set(0)
    return mask_values


def draw_tile_size(key, part):
    size_key = jax.random.fold_in(key, 37)
    sizes = jax.random.randint(size_key, (NTILES,), TILE // 2, TILE + 1)
    sizes = sizes.at[0].set(TILE)
    sizes = sizes.at[1].set(TILE // 2)
    return sizes.astype(jnp.int32)


def levels(key, dims, pieces, smallest, high):
    gain = 1.0
    for dim, parts in pieces:
        draws = jax.random.uniform(jax.random.fold_in(jax.random.fold_in(key, 6), dim), (parts,), jnp.float32, smallest / len(pieces), high / len(pieces))
        gain = gain * jnp.repeat(jnp.exp(draws), dims[dim] // parts).reshape((-1,) + (1,) * (len(dims) - 1 - dim))
    return gain


def centred(rng, extent, spread, most, pieces=(), kind=jnp.bfloat16):
    values = spread * jax.random.normal(rng, extent, jnp.float32)
    if pieces:
        values = values * levels(rng, extent, pieces, -0.22, 0.18)
    return jnp.clip(values, -most, most).astype(kind)


def setup_inputs(seed: int = 0) -> dict:
    splits = jax.random.split(jax.random.key(seed), 5)
    return {
        "amplitudes": centred(splits[0], (ROWS, NCD), 1.0, 6.0, ((0, 1024),)),
        "integrals": centred(splits[1], (NCD, NAB), (NCD // 2) ** -0.5, 0.0390625, ((0, 64), (1, 16))),
        "tile_mask": draw_tile_mask(jax.random.fold_in(splits[4], 71), 0),
        "tile_size": draw_tile_size(jax.random.fold_in(splits[4], 71), 0),
    }


def reference(amplitudes, integrals, tile_mask, tile_size):
    width = amplitudes.shape[1]
    column = jnp.arange(width, dtype=jnp.int32)
    tile_of = column // TILE
    column_live = (column % TILE) < tile_size[tile_of]
    group = math.gcd(DOMAINS, 64)
    amp_blocks = amplitudes.reshape(DOMAINS // group, group * ROWS_DEV, width)
    mask_blocks = tile_mask.reshape(DOMAINS // group, group, NTILES)

    def one_block(pair):
        amp_rows, mask_rows = pair
        domain_live = mask_rows[:, tile_of] == 1
        domain_live = jnp.repeat(domain_live, ROWS_DEV, axis=0)
        live = domain_live & column_live[None, :]
        masked = jnp.where(live, amp_rows, jnp.zeros_like(amp_rows))
        return jnp.dot(masked, integrals, preferred_element_type=jnp.float32).astype(jnp.bfloat16)

    result = lax.map(one_block, (amp_blocks, mask_blocks))
    return result.reshape(ROWS, NAB)
```

```python
import jax
import jax.numpy as jnp
from jax import lax
from jax.experimental import pallas as pl
from jax.experimental.pallas import tpu as pltpu
from jax.sharding import Mesh, PartitionSpec as P

NX, NZH, NZL, NY, NC = 4, 4, 4, 8, 2
NZ = NZH * NZL
NCHIP = NX * NY
NSTEP = 32
MESH = pl.DeviceIdType.MESH


def kernel(mask_ref, size_ref, amp_ref, int_ref, out_ref,
           am, a2, bb, cb, rxp, rxm, ryp, rym, sb, so,
           a_send, a_recv, a_loc, sib_send, sib_recv, b_send, b_recv,
           z_send, z_recv, x_send, x_recv, y_send, y_recv, o_send, o_recv):
    x = lax.axis_index("x")
    zh = lax.axis_index("zh")
    zl = lax.axis_index("zl")
    y = lax.axis_index("y")
    c = lax.axis_index("c")
    z = zh * NZL + zl
    me = x * NY + y
    other = 1 - c

    barrier = pltpu.get_barrier_semaphore()

    def greet(i, _):
        xx = lax.rem(x + i // NY, NX)
        yy = lax.rem(y + lax.rem(i, NY), NY)
        pl.semaphore_signal(barrier, inc=1, device_id={"x": xx, "y": yy}, device_id_type=MESH)
        return 0

    lax.fori_loop(1, NCHIP, greet, 0)
    for dx in range(NX):
        pl.semaphore_signal(barrier, inc=1, device_id={"x": lax.rem(x + dx, NX), "c": other}, device_id_type=MESH)
    zup = lax.rem(z + 1, NZ)
    zdn = lax.rem(z + NZ - 1, NZ)
    up = {"zh": zup // NZL, "zl": lax.rem(zup, NZL)}
    dn = {"zh": zdn // NZL, "zl": lax.rem(zdn, NZL)}
    pl.semaphore_signal(barrier, inc=1, device_id=up, device_id_type=MESH)
    pl.semaphore_signal(barrier, inc=1, device_id=dn, device_id_type=MESH)

    lane = lax.broadcasted_iota(jnp.int32, (8, 128), 1)

    def live(q, _):
        for t in range(12):
            tile = q * 12 + t
            limit = jnp.where(mask_ref[0, tile] == 1, size_ref[tile], 0)
            col = pl.multiple_of(tile * 128, 128)
            v = amp_ref[:, pl.ds(col, 128)].astype(jnp.float32)
            am[q, :, t * 128:(t + 1) * 128] = jnp.where(lane < limit, v, 0.0).astype(jnp.bfloat16)
        return 0

    lax.fori_loop(0, NCHIP, live, 0)
    pl.semaphore_wait(barrier, NCHIP - 1 + NX + 2)

    jb = lax.rem(x, 2)
    cdst = x // 2
    stay = (x == zl) & (c == cdst)

    def b_src(h):
        return int_ref.at[h * 192:(h + 1) * 192, :]

    @pl.when(stay)
    def _():
        for h in range(4):
            pltpu.make_async_copy(b_src(h), bb.at[jb, zh, c * 4 + h], b_recv.at[jb, c * 4 + h]).start()

    def b_copy(h):
        return pltpu.make_async_remote_copy(
            src_ref=b_src(h), dst_ref=bb.at[jb, zh, c * 4 + h],
            send_sem=b_send.at[h], recv_sem=b_recv.at[jb, c * 4 + h],
            device_id={"x": zl, "c": cdst}, device_id_type=MESH)

    @pl.when(jnp.logical_not(stay))
    def _():
        for h in range(4):
            b_copy(h).start()

    def a_copy(i):
        xx = lax.rem(x + i // NY, NX)
        yy = lax.rem(y + lax.rem(i, NY), NY)
        return pltpu.make_async_remote_copy(
            src_ref=am.at[xx * NY + yy], dst_ref=a2.at[c, pl.ds(pl.multiple_of(me * 8, 8), 8), :],
            send_sem=a_send.at[i], recv_sem=a_recv.at[i],
            device_id={"x": xx, "y": yy}, device_id_type=MESH)

    def a_start(i, _):
        a_copy(i).start()
        return 0

    lax.fori_loop(1, NCHIP, a_start, 0)
    a_own = pltpu.make_async_copy(am.at[me], a2.at[c, pl.ds(pl.multiple_of(me * 8, 8), 8), :], a_loc)
    a_own.start()

    sib_copy = pltpu.make_async_remote_copy(
        src_ref=a2.at[c], dst_ref=a2.at[c], send_sem=sib_send, recv_sem=sib_recv,
        device_id={"c": other}, device_id_type=MESH)

    def a_finish():
        def a_wait(i, _):
            a_copy(i).wait_recv()
            return 0
        lax.fori_loop(1, NCHIP, a_wait, 0)
        a_own.wait()
        sib_copy.start()

    p = lax.rem(z - x + NZ, NZL)
    sp = lax.rem((z - x + NZ) // NZL, NZH)
    dm = lax.rem(NZL - p, NZL)

    def z_parts(n, way):
        j = n // 16
        k = lax.rem(n, 16) // 8
        ch = lax.rem(n, 8)
        if way == 0:
            s = lax.rem(sp - k + NZH, NZH)
            sends = jnp.logical_not((p == 3) & (k == 1) & (ch >= 4))
        else:
            s = lax.rem(sp + jnp.where(p == 0, 0, 1) + k, NZH)
            sends = jnp.logical_not((p == 1) & (k == 1) & (ch < 4))
        copy = pltpu.make_async_remote_copy(
            src_ref=bb.at[j, s, ch], dst_ref=bb.at[j, s, ch],
            send_sem=z_send.at[way, n], recv_sem=z_recv.at[way, j, s, ch],
            device_id=up if way == 0 else dn, device_id_type=MESH)
        return j, k, s, ch, sends, copy

    def z_step(n, way):
        @pl.when((n >= 0) & (n < NSTEP))
        def _():
            j, k, s, ch, sends, copy = z_parts(n, way)
            own = (p == 0) & (k == 0)

            @pl.when(jnp.logical_not(own))
            def _():
                copy.wait_recv()

            if way == 0:
                @pl.when(own)
                def _():
                    pltpu.make_async_copy(bb.at[j, s, ch], bb.at[j, s, ch], b_recv.at[j, ch]).wait()

            @pl.when(sends)
            def _():
                copy.start()

    def z_slots(lo, hi):
        def slot(t, _):
            z_step(t - p, 0)
            z_step(t - dm, 1)
            return 0
        lax.fori_loop(lo, hi, slot, 0)

    def z_far(j):
        @pl.when(p == 0)
        def _():
            s = lax.rem(sp + 2, NZH)
            for ch in range(8):
                way = 0 if ch < 4 else 1
                pltpu.make_async_copy(bb.at[j, s, ch], bb.at[j, s, ch], z_recv.at[way, j, s, ch]).wait()

    def product(j):
        for h in range(2):
            rhs = jnp.concatenate([bb[j, 2 * h].reshape(1536, 128), bb[j, 2 * h + 1].reshape(1536, 128)], axis=1)
            for cc in range(2):
                part = jnp.dot(a2[cc], rhs, preferred_element_type=jnp.float32)
                cb[j, :, :, cc, :, h * 256:(h + 1) * 256] = part.reshape(NX, NY, 8, 256)

    xs = [lax.rem(x + d, NX) for d in range(NX)]
    ys = [lax.rem(y + d, NY) for d in range(NY)]
    right, left = {"x": xs[1]}, {"x": xs[3]}
    above, below = {"y": ys[1]}, {"y": ys[7]}

    def x_copy(j, way, m):
        if way == 0:
            src = (cb.at[j, xs[2], 0:4], cb.at[j, xs[1], 4:8], cb.at[j, xs[1], 0:4])[m]
        else:
            src = (cb.at[j, xs[2], 4:8], cb.at[j, xs[3], 0:4], cb.at[j, xs[3], 4:8])[m]
        return pltpu.make_async_remote_copy(
            src_ref=src, dst_ref=(rxp, rxm)[way].at[j, m],
            send_sem=x_send.at[j, way, m], recv_sem=x_recv.at[j, way, m],
            device_id=(right, left)[way], device_id_type=MESH)

    def y_copy(j, way, m):
        row = ys[4 - m] if way == 0 else ys[4 + m]
        if m == 0:
            src = cb.at[j, x, row, way]
            dst = (ryp, rym)[way].at[j, 0, way]
        else:
            src = cb.at[j, x, row]
            dst = (ryp, rym)[way].at[j, m]
        return pltpu.make_async_remote_copy(
            src_ref=src, dst_ref=dst,
            send_sem=y_send.at[j, way, m], recv_sem=y_recv.at[j, way, m],
            device_id=(above, below)[way], device_id_type=MESH)

    def o_copy(j):
        return pltpu.make_async_remote_copy(
            src_ref=sb.at[j], dst_ref=so.at[j], send_sem=o_send.at[j], recv_sem=o_recv.at[j],
            device_id={"c": other}, device_id_type=MESH)

    def x_first(j):
        for m in range(2):
            x_copy(j, 0, m).start()
            x_copy(j, 1, m).start()

    def x_second(j):
        x_copy(j, 0, 0).wait_recv()
        cb[j, xs[1], 0:4] = cb[j, xs[1], 0:4] + rxp[j, 0]
        x_copy(j, 0, 2).start()
        x_copy(j, 1, 0).wait_recv()
        cb[j, xs[3], 4:8] = cb[j, xs[3], 4:8] + rxm[j, 0]
        x_copy(j, 1, 2).start()

    def x_last(j):
        for m in range(1, 3):
            x_copy(j, 0, m).wait_recv()
            x_copy(j, 1, m).wait_recv()
        cb[j, x, 0:4] = cb[j, x, 0:4] + rxp[j, 2] + rxm[j, 1]
        cb[j, x, 4:8] = cb[j, x, 4:8] + rxp[j, 1] + rxm[j, 2]
        y_copy(j, 0, 0).start()
        y_copy(j, 1, 0).start()

    def y_next(j, m):
        for way in range(2):
            row = ys[4 - m] if way == 0 else ys[4 + m]
            buf = (ryp, rym)[way]
            y_copy(j, way, m - 1).wait_recv()
            if m == 1:
                cb[j, x, row, way] = cb[j, x, row, way] + buf[j, 0, way]
            else:
                cb[j, x, row] = cb[j, x, row] + buf[j, m - 1]
            y_copy(j, way, m).start()

    def y_last(j):
        y_copy(j, 0, 3).wait_recv()
        y_copy(j, 1, 3).wait_recv()
        sb[j] = (cb[j, x, y, other] + ryp[j, 3, other] + rym[j, 3, other]).astype(jnp.bfloat16)
        o_copy(j).start()
        mine = (cb[j, x, y, c] + ryp[j, 3, c] + rym[j, 3, c]).astype(jnp.bfloat16)
        out_ref[:, pl.ds(pl.multiple_of((2 * c + j) * 512, 512), 512)] = mine

    def tail(j):
        return [lambda: x_second(j), lambda: x_last(j)] + [
            (lambda m=m: y_next(j, m)) for m in range(1, 4)] + [lambda: y_last(j)]

    z_slots(0, 14)
    a_finish()
    z_slots(14, 19)
    z_far(0)
    sib_copy.wait_recv()
    product(0)
    x_first(0)
    at = 19
    for step, event in zip((5, 3, 2, 2, 2, 2), tail(0)):
        z_slots(at, at + step)
        at += step
        event()
    z_slots(at, NSTEP + 3)
    z_far(1)
    product(1)
    x_first(1)
    for event in tail(1):
        event()

    for j in range(2):
        o_copy(j).wait_recv()
        out_ref[:, pl.ds(pl.multiple_of((2 * other + j) * 512, 512), 512)] = so[j]

    def a_left(i, _):
        a_copy(i).wait_send()
        return 0

    lax.fori_loop(1, NCHIP, a_left, 0)
    sib_copy.wait_send()

    @pl.when(jnp.logical_not(stay))
    def _():
        for h in range(4):
            b_copy(h).wait_send()

    def z_left(n, _):
        for way in range(2):
            parts = z_parts(n, way)

            @pl.when(parts[4])
            def _():
                parts[5].wait_send()
        return 0

    lax.fori_loop(0, NSTEP, z_left, 0)
    for j in range(2):
        for way in range(2):
            for m in range(3):
                x_copy(j, way, m).wait_send()
            for m in range(4):
                y_copy(j, way, m).wait_send()
        o_copy(j).wait_send()


def body(amplitudes, integrals, tile_mask, tile_size):
    dma = pltpu.SemaphoreType.DMA
    f32, bf16 = jnp.float32, jnp.bfloat16
    return pl.pallas_call(
        kernel,
        out_shape=jax.ShapeDtypeStruct((8, 2048), bf16),
        in_specs=[pl.BlockSpec(memory_space=pltpu.SMEM)] * 2 + [pl.BlockSpec(memory_space=pltpu.VMEM)] * 2,
        out_specs=pl.BlockSpec(memory_space=pltpu.VMEM),
        scratch_shapes=[
            pltpu.VMEM((NCHIP, 8, 1536), bf16),
            pltpu.VMEM((2, 256, 1536), bf16),
            pltpu.VMEM((2, NZH, 8, 192, 128), bf16),
            pltpu.VMEM((2, NX, NY, 2, 8, 512), f32),
            pltpu.VMEM((2, 3, 4, 2, 8, 512), f32),
            pltpu.VMEM((2, 3, 4, 2, 8, 512), f32),
            pltpu.VMEM((2, 4, 2, 8, 512), f32),
            pltpu.VMEM((2, 4, 2, 8, 512), f32),
            pltpu.VMEM((2, 8, 512), bf16),
            pltpu.VMEM((2, 8, 512), bf16),
            dma((NCHIP,)), dma((NCHIP,)), dma(()), dma(()), dma(()),
            dma((4,)), dma((2, 8)),
            dma((2, NSTEP)), dma((2, 2, NZH, 8)),
            dma((2, 2, 3)), dma((2, 2, 3)),
            dma((2, 2, 4)), dma((2, 2, 4)),
            dma((2,)), dma((2,)),
        ],
        compiler_params=pltpu.CompilerParams(collective_id=0, has_side_effects=True),
    )(tile_mask, tile_size, amplitudes, integrals)


def solution(mesh):
    axes = ("x", "zh", "zl", "y", "c")
    fine = Mesh(mesh.devices.reshape(NX, NZH, NZL, NY, NC), axes)
    return jax.shard_map(
        body,
        mesh=fine,
        in_specs=(P(axes, None), P(("zl", "y", "c"), ("x", "zh")), P(axes, None), P()),
        out_specs=P(axes, None),
        check_vma=False,
    )
```

```python
import jax
import jax.numpy as jnp
from jax import lax
from jax.experimental import pallas as pl
from jax.experimental.pallas import tpu as pltpu
from jax.sharding import Mesh, PartitionSpec as P

NX, NZH, NZL, NY, NC = 4, 4, 4, 8, 2
NZ = NZH * NZL
NCHIP = NX * NY
NPIECE = 4
FAR = NZ // 2
NSTEP = NPIECE * FAR
ROUNDS = NZH
MESH = pl.DeviceIdType.MESH


def kernel(mask_ref, size_ref, amp_ref, int_ref, out_ref,
           am, a2, bb, ca, cb, rxp, rxm, ryp, rym, fa, fb, sb, so,
           a_send, a_recv, a_loc, sib_send, sib_recv, b_send, b_recv,
           z_send, z_recv, x_send, x_recv, y_send, y_recv, fa_send, fa_recv, fb_send, fb_recv, o_send, o_recv):
    x = lax.axis_index("x")
    zh = lax.axis_index("zh")
    zl = lax.axis_index("zl")
    y = lax.axis_index("y")
    c = lax.axis_index("c")
    z = zh * NZL + zl
    me = x * NY + y
    other = 1 - c

    barrier = pltpu.get_barrier_semaphore()

    def greet(i, _):
        xx = lax.rem(x + i // NY, NX)
        yy = lax.rem(y + lax.rem(i, NY), NY)
        pl.semaphore_signal(barrier, inc=1, device_id={"x": xx, "y": yy}, device_id_type=MESH)
        return 0

    lax.fori_loop(1, NCHIP, greet, 0)
    for dx in range(NX):
        pl.semaphore_signal(barrier, inc=1, device_id={"x": lax.rem(x + dx, NX), "c": other}, device_id_type=MESH)
    zup = lax.rem(z + 1, NZ)
    zdn = lax.rem(z + NZ - 1, NZ)
    up = {"zh": zup // NZL, "zl": lax.rem(zup, NZL)}
    dn = {"zh": zdn // NZL, "zl": lax.rem(zdn, NZL)}
    pl.semaphore_signal(barrier, inc=1, device_id=up, device_id_type=MESH)
    pl.semaphore_signal(barrier, inc=1, device_id=dn, device_id_type=MESH)

    pl.semaphore_wait(barrier, NCHIP - 1 + NX + 2)

    jb = lax.rem(x, 2)
    cdst = x // 2

    def b_src(h, half):
        return int_ref.at[(2 * h + half) * 192:(2 * h + half + 1) * 192, :]

    def b_copy(h, half):
        return pltpu.make_async_remote_copy(
            src_ref=b_src(h, half), dst_ref=bb.at[jb, zh, zl, half],
            send_sem=b_send.at[h, half], recv_sem=b_recv.at[jb, half],
            device_id={"x": 2 * c + h, "c": cdst}, device_id_type=MESH)

    def b_stays(h):
        return x == 2 * c + h

    for half in range(2):
        for h in range(2):
            @pl.when(b_stays(h))
            def _():
                pltpu.make_async_copy(b_src(h, half), bb.at[jb, zh, zl, half], b_recv.at[jb, half]).start()

            @pl.when(jnp.logical_not(b_stays(h)))
            def _():
                b_copy(h, half).start()

    lane = lax.broadcasted_iota(jnp.int32, (8, 128), 1)

    def live(q, _):
        for t in range(12):
            tile = ((t // 3) * 2 * NY + 2 * lax.rem(q, NY)) * 6 + (q // NY) * 3 + t % 3
            limit = jnp.where(mask_ref[0, tile] == 1, size_ref[tile], 0)
            col = pl.multiple_of(tile * 128, 128)
            v = amp_ref[:, pl.ds(col, 128)].astype(jnp.float32)
            am[q, :, t * 128:(t + 1) * 128] = jnp.where(lane < limit, v, 0.0).astype(jnp.bfloat16)
        return 0

    lax.fori_loop(0, NCHIP, live, 0)
    def a_copy(i):
        xx = lax.rem(x + i // NY, NX)
        yy = lax.rem(y + lax.rem(i, NY), NY)
        return pltpu.make_async_remote_copy(
            src_ref=am.at[xx * NY + yy], dst_ref=a2.at[c, pl.ds(pl.multiple_of(me * 8, 8), 8), :],
            send_sem=a_send.at[i], recv_sem=a_recv.at[i],
            device_id={"x": xx, "y": yy}, device_id_type=MESH)

    def a_start(i, _):
        a_copy(i).start()
        return 0

    lax.fori_loop(1, NCHIP, a_start, 0)
    a_own = pltpu.make_async_copy(am.at[me], a2.at[c, pl.ds(pl.multiple_of(me * 8, 8), 8), :], a_loc)
    a_own.start()

    sib_copy = pltpu.make_async_remote_copy(
        src_ref=a2.at[c], dst_ref=a2.at[c], send_sem=sib_send, recv_sem=sib_recv,
        device_id={"c": other}, device_id_type=MESH)

    def a_finish():
        def a_wait(i, _):
            a_copy(i).wait_recv()
            return 0
        lax.fori_loop(1, NCHIP, a_wait, 0)
        a_own.wait()
        sib_copy.start()

    def z_parts(n, way):
        d = n // NPIECE
        i = lax.rem(n, NPIECE)
        zs = lax.rem(z + (NZ - d if way == 0 else d), NZ)
        ref = bb.at[lax.rem(i, 2), zs // NZL, lax.rem(zs, NZL), i // 2]
        return d, i, ref

    def z_copy(n, way):
        _, _, ref = z_parts(n, way)
        return pltpu.make_async_remote_copy(
            src_ref=ref, dst_ref=ref, send_sem=z_send.at[way, n], recv_sem=z_recv.at[way, n + NPIECE],
            device_id=up if way == 0 else dn, device_id_type=MESH)

    def z_arrive(n, way):
        _, _, ref = z_parts(n, way)
        pltpu.make_async_copy(ref, ref, z_recv.at[way, n]).wait()

    def z_passes(n, way):
        d, i, _ = z_parts(n, way)
        near = (i < NPIECE // 2) if way == 0 else (i >= NPIECE // 2)
        return (d < FAR - 1) | near

    def z_slots(lo, hi):
        def slot(n, _):
            @pl.when(n < NPIECE)
            def _():
                _, i, ref = z_parts(n, 0)
                pltpu.make_async_copy(ref, ref, b_recv.at[lax.rem(i, 2), i // 2]).wait()

            for way in range(2):
                @pl.when(n >= NPIECE)
                def _():
                    z_arrive(n, way)

                @pl.when(z_passes(n, way))
                def _():
                    z_copy(n, way).start()
            return 0
        lax.fori_loop(lo, hi, slot, 0)

    def z_far():
        for i in range(NPIECE):
            z_arrive(NSTEP + i, 0 if i < NPIECE // 2 else 1)

    side = jnp.where(zl < NZL // 2, NZH - 1, 1)
    block = [zh, lax.rem(zh + side, NZH), lax.rem(zh + NZH - side, NZH), lax.rem(zh + NZH // 2, NZH)]

    def product(r):
        rhs = jnp.concatenate([bb[0, block[r]].reshape(1536, 128), bb[1, block[r]].reshape(1536, 128)], axis=1)
        for cc in range(2):
            part = jnp.dot(a2[cc], rhs, preferred_element_type=jnp.float32).reshape(NX, NY, 8, 256)
            ca[r, :, :, cc] = part[:, :, :, :128]
            for xx in range(NX):
                cb[r, :, xx, cc] = part[xx, :, :, 128:]

    xs = [lax.rem(x + d, NX) for d in range(NX)]
    ys = [lax.rem(y + d, NY) for d in range(NY)]

    def x_copy(j, way, m):
        if way == 0:
            src = (ca.at[j, xs[2], 0:4], ca.at[j, xs[1], 4:8], ca.at[j, xs[1], 0:4])[m]
        else:
            src = (ca.at[j, xs[2], 4:8], ca.at[j, xs[3], 0:4], ca.at[j, xs[3], 4:8])[m]
        return pltpu.make_async_remote_copy(
            src_ref=src, dst_ref=(rxp, rxm)[way].at[j, m],
            send_sem=x_send.at[j, way, m], recv_sem=x_recv.at[j, way, m],
            device_id={"x": xs[1] if way == 0 else xs[3]}, device_id_type=MESH)

    def y_copy(j, way, m):
        row = ys[4 - m] if way == 0 else ys[4 + m]
        buf = (ryp, rym)[way]
        if m == 0:
            src = cb.at[j, row, 2 * way:2 * way + 2]
            dst = buf.at[j, 0, 2 * way:2 * way + 2]
        else:
            src = cb.at[j, row]
            dst = buf.at[j, m]
        return pltpu.make_async_remote_copy(
            src_ref=src, dst_ref=dst,
            send_sem=y_send.at[j, way, m], recv_sem=y_recv.at[j, way, m],
            device_id={"y": ys[1] if way == 0 else ys[7]}, device_id_type=MESH)

    def fa_copy(j, d):
        return pltpu.make_async_remote_copy(
            src_ref=ca.at[j, x, ys[d]], dst_ref=fa.at[j, d], send_sem=fa_send.at[j, d], recv_sem=fa_recv.at[j, d],
            device_id={"y": ys[d]}, device_id_type=MESH)

    def fb_copy(j, d):
        return pltpu.make_async_remote_copy(
            src_ref=cb.at[j, y, xs[d]], dst_ref=fb.at[j, d], send_sem=fb_send.at[j, d], recv_sem=fb_recv.at[j, d],
            device_id={"x": xs[d]}, device_id_type=MESH)

    def o_copy(j):
        return pltpu.make_async_remote_copy(
            src_ref=sb.at[j], dst_ref=so.at[j], send_sem=o_send.at[j], recv_sem=o_recv.at[j],
            device_id={"c": other}, device_id_type=MESH)

    def first(j):
        product(j)
        y_copy(j, 0, 0).start()
        y_copy(j, 1, 0).start()
        for m in range(2):
            x_copy(j, 0, m).start()
            x_copy(j, 1, m).start()

    def x_second(j):
        x_copy(j, 0, 0).wait_recv()
        ca[j, xs[1], 0:4] = ca[j, xs[1], 0:4] + rxp[j, 0]
        x_copy(j, 0, 2).start()
        x_copy(j, 1, 0).wait_recv()
        ca[j, xs[3], 4:8] = ca[j, xs[3], 4:8] + rxm[j, 0]
        x_copy(j, 1, 2).start()

    def x_last(j):
        for m in range(1, 3):
            x_copy(j, 0, m).wait_recv()
            x_copy(j, 1, m).wait_recv()
        ca[j, x, 0:4] = ca[j, x, 0:4] + rxp[j, 2] + rxm[j, 1]
        ca[j, x, 4:8] = ca[j, x, 4:8] + rxp[j, 1] + rxm[j, 2]
        for d in (4, 3, 5, 2, 6, 1, 7):
            fa_copy(j, d).start()

    def y_next(j, m):
        for way in range(2):
            row = ys[4 - m] if way == 0 else ys[4 + m]
            buf = (ryp, rym)[way]
            y_copy(j, way, m - 1).wait_recv()
            if m == 1:
                part = slice(2 * way, 2 * way + 2)
                cb[j, row, part] = cb[j, row, part] + buf[j, 0, part]
            else:
                cb[j, row] = cb[j, row] + buf[j, m - 1]
            y_copy(j, way, m).start()

    def y_last(j):
        y_copy(j, 0, 3).wait_recv()
        y_copy(j, 1, 3).wait_recv()
        cb[j, y] = cb[j, y] + ryp[j, 3] + rym[j, 3]
        for d in (2, 1, 3):
            fb_copy(j, d).start()

    def finish(j):
        for d in range(1, NY):
            fa_copy(j, d).wait_recv()
        for d in range(1, NX):
            fb_copy(j, d).wait_recv()

        def rows(core):
            left = ca[j, x, y, core]
            for d in range(1, NY):
                left = left + fa[j, d, core]
            right = cb[j, y, x, core]
            for d in range(1, NX):
                right = right + fb[j, d, core]
            return left.astype(jnp.bfloat16), right.astype(jnp.bfloat16)

        left, right = rows(other)
        sb[j, :, :128] = left
        sb[j, :, 128:] = right
        o_copy(j).start()
        store(j, c, *rows(c))

    def store(j, core, left, right):
        for half, value in enumerate((left, right)):
            col = ((2 * core + half) * NZH + block[j]) * 128
            out_ref[:, pl.ds(pl.multiple_of(col, 128), 128)] = value

    def e1(r):
        y_next(r, 1)
        x_second(r)

    def e3(r):
        x_last(r)
        y_next(r, 3)

    z_slots(0, 24)
    a_finish()
    z_slots(24, 27)
    sib_copy.wait_recv()
    first(0)
    z_slots(27, 29)
    first(1)
    e1(0)
    z_slots(29, 31)
    y_next(0, 2)
    e1(1)
    z_slots(31, 32)
    first(2)
    e3(0)
    z_far()
    first(3)
    y_next(1, 2)
    y_last(0)
    e1(2)
    e1(3)
    e3(1)
    y_next(2, 2)
    y_next(3, 2)
    y_last(1)
    finish(0)
    e3(2)
    e3(3)
    finish(1)
    y_last(2)
    y_last(3)
    finish(2)
    finish(3)

    for j in range(ROUNDS):
        o_copy(j).wait_recv()
        store(j, other, so[j, :, :128], so[j, :, 128:])

    def a_left(i, _):
        a_copy(i).wait_send()
        return 0

    lax.fori_loop(1, NCHIP, a_left, 0)
    sib_copy.wait_send()

    for h in range(2):
        @pl.when(jnp.logical_not(b_stays(h)))
        def _():
            for half in range(2):
                b_copy(h, half).wait_send()

    def z_left(n, _):
        for way in range(2):
            @pl.when(z_passes(n, way))
            def _():
                z_copy(n, way).wait_send()
        return 0

    lax.fori_loop(0, NSTEP, z_left, 0)
    for j in range(ROUNDS):
        for way in range(2):
            for m in range(3):
                x_copy(j, way, m).wait_send()
            for m in range(4):
                y_copy(j, way, m).wait_send()
        for d in range(1, NY):
            fa_copy(j, d).wait_send()
        for d in range(1, NX):
            fb_copy(j, d).wait_send()
        o_copy(j).wait_send()


def body(amplitudes, integrals, tile_mask, tile_size):
    dma = pltpu.SemaphoreType.DMA
    f32, bf16 = jnp.float32, jnp.bfloat16
    return pl.pallas_call(
        kernel,
        out_shape=jax.ShapeDtypeStruct((8, 2048), bf16),
        in_specs=[pl.BlockSpec(memory_space=pltpu.SMEM)] * 2 + [pl.BlockSpec(memory_space=pltpu.VMEM)] * 2,
        out_specs=pl.BlockSpec(memory_space=pltpu.VMEM),
        scratch_shapes=[
            pltpu.VMEM((NCHIP, 8, 1536), bf16),
            pltpu.VMEM((2, 256, 1536), bf16),
            pltpu.VMEM((2, NZH, NZL, 2, 192, 128), bf16),
            pltpu.VMEM((ROUNDS, NX, NY, 2, 8, 128), f32),
            pltpu.VMEM((ROUNDS, NY, NX, 2, 8, 128), f32),
            pltpu.VMEM((ROUNDS, 3, 4, 2, 8, 128), f32),
            pltpu.VMEM((ROUNDS, 3, 4, 2, 8, 128), f32),
            pltpu.VMEM((ROUNDS, 4, NX, 2, 8, 128), f32),
            pltpu.VMEM((ROUNDS, 4, NX, 2, 8, 128), f32),
            pltpu.VMEM((ROUNDS, NY, 2, 8, 128), f32),
            pltpu.VMEM((ROUNDS, NX, 2, 8, 128), f32),
            pltpu.VMEM((ROUNDS, 8, 256), bf16),
            pltpu.VMEM((ROUNDS, 8, 256), bf16),
            dma((NCHIP,)), dma((NCHIP,)), dma(()), dma(()), dma(()),
            dma((2, 2)), dma((2, 2)),
            dma((2, NSTEP)), dma((2, NSTEP + NPIECE)),
            dma((ROUNDS, 2, 3)), dma((ROUNDS, 2, 3)),
            dma((ROUNDS, 2, 4)), dma((ROUNDS, 2, 4)),
            dma((ROUNDS, NY)), dma((ROUNDS, NY)), dma((ROUNDS, NX)), dma((ROUNDS, NX)),
            dma((ROUNDS,)), dma((ROUNDS,)),
        ],
        compiler_params=pltpu.CompilerParams(collective_id=0, has_side_effects=True),
    )(tile_mask, tile_size, amplitudes, integrals)


def solution(mesh):
    axes = ("x", "zh", "zl", "y", "c")
    fine = Mesh(mesh.devices.reshape(NX, NZH, NZL, NY, NC), axes)
    return jax.shard_map(
        body,
        mesh=fine,
        in_specs=(P(axes, None), P(("zl", "y", "c"), ("x", "zh")), P(axes, None), P()),
        out_specs=P(axes, None),
        check_vma=False,
    )
```

```python
import jax
import jax.numpy as jnp
from jax import lax
from jax.experimental import pallas as pl
from jax.experimental.pallas import tpu as pltpu
from jax.sharding import Mesh, PartitionSpec as P

NX, NZH, NZL, NY, NC = 4, 4, 4, 8, 2
NZ = NZH * NZL
NCHIP = NX * NY
NPIECE = 4
FAR = NZ // 2
NSTEP = NPIECE * FAR
ROUNDS = NZH
MIXED = 2
MESH = pl.DeviceIdType.MESH


def kernel(mask_ref, size_ref, amp_ref, int_ref, out_ref,
           am, a2, bb, ca, rxp, rxm, fa, cb, ryp, rym, fb, sb, so,
           a_send, a_recv, a_loc, sib_send, sib_recv, b_send, b_recv,
           z_send, z_recv, x_send, x_recv, y_send, y_recv,
           ring_send, ring_recv, fb_send, fb_recv, o_send, o_recv, entered):
    x = lax.axis_index("x")
    zh = lax.axis_index("zh")
    zl = lax.axis_index("zl")
    y = lax.axis_index("y")
    c = lax.axis_index("c")
    z = zh * NZL + zl
    me = x * NY + y
    other = 1 - c

    barrier = pltpu.get_barrier_semaphore()

    for dy in range(1, NY):
        pl.semaphore_signal(barrier, inc=1, device_id={"y": lax.rem(y + dy, NY)}, device_id_type=MESH)
    for dx in range(NX):
        xx = lax.rem(x + dx, NX)
        if dx:
            pl.semaphore_signal(barrier, inc=1, device_id={"x": xx}, device_id_type=MESH)
        pl.semaphore_signal(barrier, inc=1, device_id={"x": xx, "c": other}, device_id_type=MESH)
    zup = lax.rem(z + 1, NZ)
    zdn = lax.rem(z + NZ - 1, NZ)
    up = {"zh": zup // NZL, "zl": lax.rem(zup, NZL)}
    dn = {"zh": zdn // NZL, "zl": lax.rem(zdn, NZL)}
    pl.semaphore_signal(barrier, inc=1, device_id=up, device_id_type=MESH)
    pl.semaphore_signal(barrier, inc=1, device_id=dn, device_id_type=MESH)

    pl.semaphore_wait(barrier, NY - 1 + 2 * NX - 1 + 2)
    for dx in range(1, NX):
        pl.semaphore_signal(entered, inc=1, device_id={"x": lax.rem(x + dx, NX)}, device_id_type=MESH)

    jb = lax.rem(x, 2)
    cdst = x // 2

    def b_src(h, part):
        return int_ref.at[(2 * h + part) * 192:(2 * h + part + 1) * 192, :]

    def b_copy(h, part):
        return pltpu.make_async_remote_copy(
            src_ref=b_src(h, part), dst_ref=bb.at[jb, z, part],
            send_sem=b_send.at[h, part], recv_sem=b_recv.at[jb, part],
            device_id={"x": 2 * c + h, "c": cdst}, device_id_type=MESH)

    def b_stays(h):
        return x == 2 * c + h

    for h in range(2):
        @pl.when(b_stays(h))
        def _():
            for part in range(2):
                pltpu.make_async_copy(b_src(h, part), bb.at[jb, z, part], b_recv.at[jb, part]).start()

    for part in range(2):
        for h in range(2):
            @pl.when(jnp.logical_not(b_stays(h)))
            def _():
                b_copy(h, part).start()

    lane = lax.broadcasted_iota(jnp.int32, (8, 128), 1)

    def live(q, _):
        for t in range(12):
            tile = ((t // 3) * 2 * NY + 2 * lax.rem(q, NY)) * 6 + (q // NY) * 3 + t % 3
            limit = jnp.where(mask_ref[0, tile] == 1, size_ref[tile], 0)
            col = pl.multiple_of(tile * 128, 128)
            v = amp_ref[:, pl.ds(col, 128)].astype(jnp.float32)
            am[q, :, t * 128:(t + 1) * 128] = jnp.where(lane < limit, v, 0.0).astype(jnp.bfloat16)
        return 0

    lax.fori_loop(0, NCHIP, live, 0)
    def a_copy(i):
        xx = lax.rem(x + i // NY, NX)
        yy = lax.rem(y + lax.rem(i, NY), NY)
        return pltpu.make_async_remote_copy(
            src_ref=am.at[xx * NY + yy], dst_ref=a2.at[c, pl.ds(pl.multiple_of(me * 8, 8), 8), :],
            send_sem=a_send.at[i], recv_sem=a_recv.at[i],
            device_id={"x": xx, "y": yy}, device_id_type=MESH)

    def a_start(i, _):
        a_copy(i).start()
        return 0

    pl.semaphore_wait(entered, NX - 1)
    lax.fori_loop(1, NCHIP, a_start, 0)
    a_own = pltpu.make_async_copy(am.at[me], a2.at[c, pl.ds(pl.multiple_of(me * 8, 8), 8), :], a_loc)
    a_own.start()

    sib_copy = pltpu.make_async_remote_copy(
        src_ref=a2.at[c], dst_ref=a2.at[c], send_sem=sib_send, recv_sem=sib_recv,
        device_id={"c": other}, device_id_type=MESH)

    def a_finish():
        def a_wait(i, _):
            a_copy(i).wait_recv()
            return 0
        lax.fori_loop(1, NCHIP, a_wait, 0)
        a_own.wait()
        sib_copy.start()

    behind = [[z] + [lax.rem(z + (NZ - d if way == 0 else d), NZ) for d in range(1, FAR + 1)] for way in range(2)]

    def z_ref(n, way):
        i = n % NPIECE
        return bb.at[i % 2, behind[way][n // NPIECE], i // 2]

    def z_copy(n, way):
        ref = z_ref(n, way)
        return pltpu.make_async_remote_copy(
            src_ref=ref, dst_ref=ref, send_sem=z_send.at[way, n], recv_sem=z_recv.at[way, n + NPIECE],
            device_id=up if way == 0 else dn, device_id_type=MESH)

    def z_arrive(n, way):
        ref = z_ref(n, way)
        pltpu.make_async_copy(ref, ref, z_recv.at[way, n]).wait()

    def z_passes(n, way):
        near = (n % NPIECE < NPIECE // 2) == (way == 0)
        return n < NSTEP - NPIECE or near

    def z_slots(lo, hi):
        for n in range(lo * NPIECE // 4, hi * NPIECE // 4):
            if n < NPIECE:
                ref = z_ref(n, 0)
                pltpu.make_async_copy(ref, ref, b_recv.at[n % 2, n // 2]).wait()
            for way in range(2):
                if n >= NPIECE:
                    z_arrive(n, way)
                if z_passes(n, way):
                    z_copy(n, way).start()

    def z_far():
        for i in range(NPIECE):
            z_arrive(NSTEP + i, 0 if i < NPIECE // 2 else 1)

    side = jnp.where(zl < NZL // 2, NZH - 1, 1)
    block = [zh, lax.rem(zh + side, NZH), lax.rem(zh + NZH - side, NZH), lax.rem(zh + NZH // 2, NZH)]

    xs = [lax.rem(x + d, NX) for d in range(NX)]
    ys = [lax.rem(y + d, NY) for d in range(NY)]

    def x_copy(r, h, way, m):
        if way == 0:
            src = (ca.at[r, h, xs[2], 0:4], ca.at[r, h, xs[1], 4:8], ca.at[r, h, xs[1], 0:4])[m]
        else:
            src = (ca.at[r, h, xs[2], 4:8], ca.at[r, h, xs[3], 0:4], ca.at[r, h, xs[3], 4:8])[m]
        return pltpu.make_async_remote_copy(
            src_ref=src, dst_ref=(rxp, rxm)[way].at[r, h, m],
            send_sem=x_send.at[r, h, way, m], recv_sem=x_recv.at[r, h, way, m],
            device_id={"x": xs[1] if way == 0 else xs[3]}, device_id_type=MESH)

    def y_copy(r, h, d):
        return pltpu.make_async_remote_copy(
            src_ref=ca.at[r, h, x, ys[d]], dst_ref=fa.at[r, h, d],
            send_sem=y_send.at[r, h, d], recv_sem=y_recv.at[r, h, d],
            device_id={"y": ys[d]}, device_id_type=MESH)

    def ring_copy(way, m):
        row = ys[4 - m] if way == 0 else ys[4 + m]
        buf = (ryp, rym)[way]
        part = slice(2 * way, 2 * way + 2) if m == 0 else slice(0, NX)
        return pltpu.make_async_remote_copy(
            src_ref=cb.at[row, part], dst_ref=buf.at[m, part],
            send_sem=ring_send.at[way, m], recv_sem=ring_recv.at[way, m],
            device_id={"y": ys[1] if way == 0 else ys[7]}, device_id_type=MESH)

    def fb_copy(d):
        return pltpu.make_async_remote_copy(
            src_ref=cb.at[y, xs[d]], dst_ref=fb.at[d], send_sem=fb_send.at[d], recv_sem=fb_recv.at[d],
            device_id={"x": xs[d]}, device_id_type=MESH)

    def ring_next(m):
        for way in range(2):
            row = ys[4 - m] if way == 0 else ys[4 + m]
            buf = (ryp, rym)[way]
            ring_copy(way, m - 1).wait_recv()
            part = slice(2 * way, 2 * way + 2) if m == 1 else slice(0, NX)
            cb[row, part] = cb[row, part] + buf[m - 1, part]
            ring_copy(way, m).start()

    def ring_last():
        ring_copy(0, 3).wait_recv()
        ring_copy(1, 3).wait_recv()
        cb[y] = cb[y] + ryp[3] + rym[3]
        for d in (2, 1, 3):
            fb_copy(d).start()

    def halves(r):
        return (0,) if r == MIXED else (0, 1)

    def o_copy(r):
        return pltpu.make_async_remote_copy(
            src_ref=sb.at[r], dst_ref=so.at[r], send_sem=o_send.at[r], recv_sem=o_recv.at[r],
            device_id={"c": other}, device_id_type=MESH)

    def first(r):
        rhs = jnp.concatenate([bb[0, pl.ds(NZL * block[r], NZL)].reshape(1536, 128), bb[1, pl.ds(NZL * block[r], NZL)].reshape(1536, 128)], axis=1)
        for cc in range(2):
            part = jnp.dot(a2[cc], rhs, preferred_element_type=jnp.float32).reshape(NX, NY, 8, 256)
            for h in halves(r):
                ca[r, h, :, :, cc] = part[:, :, :, h * 128:(h + 1) * 128]
            if r == MIXED:
                for xx in range(NX):
                    cb[:, xx, cc] = part[xx, :, :, 128:]
        if r == MIXED:
            ring_copy(0, 0).start()
            ring_copy(1, 0).start()
        for h in halves(r):
            for m in range(2):
                x_copy(r, h, 0, m).start()
                x_copy(r, h, 1, m).start()

    def second(r):
        for h in halves(r):
            x_copy(r, h, 0, 0).wait_recv()
            ca[r, h, xs[1], 0:4] = ca[r, h, xs[1], 0:4] + rxp[r, h, 0]
            x_copy(r, h, 0, 2).start()
            x_copy(r, h, 1, 0).wait_recv()
            ca[r, h, xs[3], 4:8] = ca[r, h, xs[3], 4:8] + rxm[r, h, 0]
            x_copy(r, h, 1, 2).start()

    def third(r):
        for h in halves(r):
            for m in range(1, 3):
                x_copy(r, h, 0, m).wait_recv()
                x_copy(r, h, 1, m).wait_recv()
            ca[r, h, x, 0:4] = ca[r, h, x, 0:4] + rxp[r, h, 2] + rxm[r, h, 1]
            ca[r, h, x, 4:8] = ca[r, h, x, 4:8] + rxp[r, h, 1] + rxm[r, h, 2]
            for d in (4, 3, 5, 2, 6, 1, 7):
                y_copy(r, h, d).start()

    def store(r, core, h, value):
        col = ((2 * core + h) * NZH + block[r]) * 128
        out_ref[:, pl.ds(pl.multiple_of(col, 128), 128)] = value

    def finish(r):
        for h in halves(r):
            for d in range(1, NY):
                y_copy(r, h, d).wait_recv()
        if r == MIXED:
            for d in range(1, NX):
                fb_copy(d).wait_recv()

        def rows(h, core):
            if h not in halves(r):
                total = cb[y, x, core]
                for d in range(1, NX):
                    total = total + fb[d, core]
                return total.astype(jnp.bfloat16)
            total = ca[r, h, x, y, core]
            for d in range(1, NY):
                total = total + fa[r, h, d, core]
            return total.astype(jnp.bfloat16)

        for h in range(2):
            sb[r, :, h * 128:(h + 1) * 128] = rows(h, other)
        o_copy(r).start()
        for h in range(2):
            store(r, c, h, rows(h, c))

    z_slots(0, 25)
    a_finish()
    z_slots(25, 26)
    sib_copy.wait_recv()
    first(0)
    z_slots(26, 28)
    first(1)
    z_slots(28, 30)
    second(0)
    z_slots(30, 32)
    first(2)
    second(1)
    third(0)
    z_far()
    first(3)
    ring_next(1)
    third(1)
    second(2)
    ring_next(2)
    second(3)
    finish(0)
    third(2)
    ring_next(3)
    finish(1)
    third(3)
    ring_last()
    finish(2)
    finish(3)

    for r in range(ROUNDS):
        o_copy(r).wait_recv()
        for h in range(2):
            store(r, other, h, so[r, :, h * 128:(h + 1) * 128])

    def a_left(i, _):
        a_copy(i).wait_send()
        return 0

    lax.fori_loop(1, NCHIP, a_left, 0)
    sib_copy.wait_send()

    for h in range(2):
        @pl.when(jnp.logical_not(b_stays(h)))
        def _():
            for part in range(2):
                b_copy(h, part).wait_send()

    for n in range(NSTEP):
        for way in range(2):
            if z_passes(n, way):
                z_copy(n, way).wait_send()
    for r in range(ROUNDS):
        for h in halves(r):
            for way in range(2):
                for m in range(3):
                    x_copy(r, h, way, m).wait_send()
            for d in range(1, NY):
                y_copy(r, h, d).wait_send()
        o_copy(r).wait_send()
    for way in range(2):
        for m in range(4):
            ring_copy(way, m).wait_send()
    for d in range(1, NX):
        fb_copy(d).wait_send()


def body(amplitudes, integrals, tile_mask, tile_size):
    dma = pltpu.SemaphoreType.DMA
    f32, bf16 = jnp.float32, jnp.bfloat16
    return pl.pallas_call(
        kernel,
        out_shape=jax.ShapeDtypeStruct((8, 2048), bf16),
        in_specs=[pl.BlockSpec(memory_space=pltpu.SMEM)] * 2 + [pl.BlockSpec(memory_space=pltpu.VMEM)] * 2,
        out_specs=pl.BlockSpec(memory_space=pltpu.VMEM),
        scratch_shapes=[
            pltpu.VMEM((NCHIP, 8, 1536), bf16),
            pltpu.VMEM((2, 256, 1536), bf16),
            pltpu.VMEM((2, NZ, 2, 192, 128), bf16),
            pltpu.VMEM((ROUNDS, 2, NX, NY, 2, 8, 128), f32),
            pltpu.VMEM((ROUNDS, 2, 3, 4, 2, 8, 128), f32),
            pltpu.VMEM((ROUNDS, 2, 3, 4, 2, 8, 128), f32),
            pltpu.VMEM((ROUNDS, 2, NY, 2, 8, 128), f32),
            pltpu.VMEM((NY, NX, 2, 8, 128), f32),
            pltpu.VMEM((4, NX, 2, 8, 128), f32),
            pltpu.VMEM((4, NX, 2, 8, 128), f32),
            pltpu.VMEM((NX, 2, 8, 128), f32),
            pltpu.VMEM((ROUNDS, 8, 256), bf16),
            pltpu.VMEM((ROUNDS, 8, 256), bf16),
            dma((NCHIP,)), dma((NCHIP,)), dma(()), dma(()), dma(()),
            dma((2, 2)), dma((2, 2)),
            dma((2, NSTEP)), dma((2, NSTEP + NPIECE)),
            dma((ROUNDS, 2, 2, 3)), dma((ROUNDS, 2, 2, 3)),
            dma((ROUNDS, 2, NY)), dma((ROUNDS, 2, NY)),
            dma((2, 4)), dma((2, 4)), dma((NX,)), dma((NX,)),
            dma((ROUNDS,)), dma((ROUNDS,)), pltpu.SemaphoreType.REGULAR,
        ],
        compiler_params=pltpu.CompilerParams(collective_id=0, has_side_effects=True),
    )(tile_mask, tile_size, amplitudes, integrals)


def solution(mesh):
    axes = ("x", "zh", "zl", "y", "c")
    fine = Mesh(mesh.devices.reshape(NX, NZH, NZL, NY, NC), axes)
    return jax.shard_map(
        body,
        mesh=fine,
        in_specs=(P(axes, None), P(("zl", "y", "c"), ("x", "zh")), P(axes, None), P()),
        out_specs=P(axes, None),
        check_vma=False,
    )
```

```python
import jax
import jax.numpy as jnp
from jax import lax
from jax.experimental import pallas as pl
from jax.experimental.pallas import tpu as pltpu
from jax.sharding import Mesh, PartitionSpec as P

NX, NZH, NZL, NY, NC = 4, 4, 4, 8, 2
NZ = NZH * NZL
NCHIP = NX * NY
NPIECE = 4
FAR = NZ // 2
NSTEP = NPIECE * FAR
ROUNDS = NZH
MIXED = 2
MESH = pl.DeviceIdType.MESH


def kernel(mask_ref, size_ref, amp_ref, int_ref, out_ref,
           am, a2, bb, ca, rxp, rxm, fa, cb, ryp, rym, fb, sb, so,
           a_send, a_recv, a_loc, sib_send, sib_recv, b_send, b_recv,
           z_send, z_recv, x_send, x_recv, y_send, y_recv,
           ring_send, ring_recv, fb_send, fb_recv, o_send, o_recv, near, far, entered):
    x = lax.axis_index("x")
    zh = lax.axis_index("zh")
    zl = lax.axis_index("zl")
    y = lax.axis_index("y")
    c = lax.axis_index("c")
    z = zh * NZL + zl
    me = x * NY + y
    other = 1 - c

    barrier = pltpu.get_barrier_semaphore()

    for dy in (1, NY - 1):
        pl.semaphore_signal(barrier, inc=1, device_id={"y": lax.rem(y + dy, NY)}, device_id_type=MESH)
    for dx in range(NX):
        xx = lax.rem(x + dx, NX)
        if dx:
            pl.semaphore_signal(barrier, inc=1, device_id={"x": xx}, device_id_type=MESH)
        pl.semaphore_signal(barrier, inc=1, device_id={"x": xx, "c": other}, device_id_type=MESH)
    zup = lax.rem(z + 1, NZ)
    zdn = lax.rem(z + NZ - 1, NZ)
    up = {"zh": zup // NZL, "zl": lax.rem(zup, NZL)}
    dn = {"zh": zdn // NZL, "zl": lax.rem(zdn, NZL)}
    pl.semaphore_signal(barrier, inc=1, device_id=up, device_id_type=MESH)
    pl.semaphore_signal(barrier, inc=1, device_id=dn, device_id_type=MESH)

    pl.semaphore_wait(barrier, 2 + 2 * NX - 1 + 2)
    for dy in (1, NY - 1):
        pl.semaphore_signal(near, inc=1, device_id={"y": lax.rem(y + dy, NY)}, device_id_type=MESH)

    jb = lax.rem(x, 2)
    cdst = x // 2

    def b_src(h, part):
        return int_ref.at[(2 * h + part) * 192:(2 * h + part + 1) * 192, :]

    def b_copy(h, part):
        return pltpu.make_async_remote_copy(
            src_ref=b_src(h, part), dst_ref=bb.at[jb, z, part],
            send_sem=b_send.at[h, part], recv_sem=b_recv.at[jb, part],
            device_id={"x": 2 * c + h, "c": cdst}, device_id_type=MESH)

    def b_stays(h):
        return x == 2 * c + h

    for h in range(2):
        @pl.when(b_stays(h))
        def _():
            for part in range(2):
                pltpu.make_async_copy(b_src(h, part), bb.at[jb, z, part], b_recv.at[jb, part]).start()

    for part in range(2):
        for h in range(2):
            @pl.when(jnp.logical_not(b_stays(h)))
            def _():
                b_copy(h, part).start()

    lane = lax.broadcasted_iota(jnp.int32, (8, 128), 1)

    def live(q, _):
        for t in range(12):
            tile = ((t // 3) * 2 * NY + 2 * lax.rem(q, NY)) * 6 + (q // NY) * 3 + t % 3
            limit = jnp.where(mask_ref[0, tile] == 1, size_ref[tile], 0)
            col = pl.multiple_of(tile * 128, 128)
            v = amp_ref[:, pl.ds(col, 128)].astype(jnp.float32)
            am[q, :, t * 128:(t + 1) * 128] = jnp.where(lane < limit, v, 0.0).astype(jnp.bfloat16)
        return 0

    lax.fori_loop(0, NCHIP, live, 0)
    def a_copy(i):
        xx = lax.rem(x + i // NY, NX)
        yy = lax.rem(y + lax.rem(i, NY), NY)
        return pltpu.make_async_remote_copy(
            src_ref=am.at[xx * NY + yy], dst_ref=a2.at[c, pl.ds(pl.multiple_of(me * 8, 8), 8), :],
            send_sem=a_send.at[i], recv_sem=a_recv.at[i],
            device_id={"x": xx, "y": yy}, device_id_type=MESH)

    def a_start(i, _):
        a_copy(i).start()
        return 0

    pl.semaphore_wait(near, 2)
    for dy in (2, NY - 2):
        pl.semaphore_signal(far, inc=1, device_id={"y": lax.rem(y + dy, NY)}, device_id_type=MESH)
    pl.semaphore_wait(far, 2)
    for dx in range(1, NX):
        pl.semaphore_signal(entered, inc=1, device_id={"x": lax.rem(x + dx, NX)}, device_id_type=MESH)
    pl.semaphore_wait(entered, NX - 1)
    lax.fori_loop(1, NCHIP, a_start, 0)
    a_own = pltpu.make_async_copy(am.at[me], a2.at[c, pl.ds(pl.multiple_of(me * 8, 8), 8), :], a_loc)
    a_own.start()

    sib_copy = pltpu.make_async_remote_copy(
        src_ref=a2.at[c], dst_ref=a2.at[c], send_sem=sib_send, recv_sem=sib_recv,
        device_id={"c": other}, device_id_type=MESH)

    def a_finish():
        def a_wait(i, _):
            a_copy(i).wait_recv()
            return 0
        lax.fori_loop(1, NCHIP, a_wait, 0)
        a_own.wait()
        sib_copy.start()

    behind = [[z] + [lax.rem(z + (NZ - d if way == 0 else d), NZ) for d in range(1, FAR + 1)] for way in range(2)]

    def z_ref(n, way):
        i = n % NPIECE
        return bb.at[i % 2, behind[way][n // NPIECE], i // 2]

    def z_copy(n, way):
        ref = z_ref(n, way)
        return pltpu.make_async_remote_copy(
            src_ref=ref, dst_ref=ref, send_sem=z_send.at[way, n], recv_sem=z_recv.at[way, n + NPIECE],
            device_id=up if way == 0 else dn, device_id_type=MESH)

    def z_arrive(n, way):
        ref = z_ref(n, way)
        pltpu.make_async_copy(ref, ref, z_recv.at[way, n]).wait()

    def z_passes(n, way):
        near = (n % NPIECE < NPIECE // 2) == (way == 0)
        return n < NSTEP - NPIECE or near

    def z_slots(lo, hi):
        for n in range(lo * NPIECE // 4, hi * NPIECE // 4):
            if n < NPIECE:
                ref = z_ref(n, 0)
                pltpu.make_async_copy(ref, ref, b_recv.at[n % 2, n // 2]).wait()
            for way in range(2):
                if n >= NPIECE:
                    z_arrive(n, way)
                if z_passes(n, way):
                    z_copy(n, way).start()

    def z_far():
        for i in range(NPIECE):
            z_arrive(NSTEP + i, 0 if i < NPIECE // 2 else 1)

    side = jnp.where(zl < NZL // 2, NZH - 1, 1)
    block = [zh, lax.rem(zh + side, NZH), lax.rem(zh + NZH - side, NZH), lax.rem(zh + NZH // 2, NZH)]

    xs = [lax.rem(x + d, NX) for d in range(NX)]
    ys = [lax.rem(y + d, NY) for d in range(NY)]

    def x_copy(r, h, way, m):
        if way == 0:
            src = (ca.at[r, h, xs[2], 0:4], ca.at[r, h, xs[1], 4:8], ca.at[r, h, xs[1], 0:4])[m]
        else:
            src = (ca.at[r, h, xs[2], 4:8], ca.at[r, h, xs[3], 0:4], ca.at[r, h, xs[3], 4:8])[m]
        return pltpu.make_async_remote_copy(
            src_ref=src, dst_ref=(rxp, rxm)[way].at[r, h, m],
            send_sem=x_send.at[r, h, way, m], recv_sem=x_recv.at[r, h, way, m],
            device_id={"x": xs[1] if way == 0 else xs[3]}, device_id_type=MESH)

    def y_copy(r, h, d):
        return pltpu.make_async_remote_copy(
            src_ref=ca.at[r, h, x, ys[d]], dst_ref=fa.at[r, h, d],
            send_sem=y_send.at[r, h, d], recv_sem=y_recv.at[r, h, d],
            device_id={"y": ys[d]}, device_id_type=MESH)

    def ring_copy(way, m):
        row = ys[4 - m] if way == 0 else ys[4 + m]
        buf = (ryp, rym)[way]
        part = slice(2 * way, 2 * way + 2) if m == 0 else slice(0, NX)
        return pltpu.make_async_remote_copy(
            src_ref=cb.at[row, part], dst_ref=buf.at[m, part],
            send_sem=ring_send.at[way, m], recv_sem=ring_recv.at[way, m],
            device_id={"y": ys[1] if way == 0 else ys[7]}, device_id_type=MESH)

    def fb_copy(d):
        return pltpu.make_async_remote_copy(
            src_ref=cb.at[y, xs[d]], dst_ref=fb.at[d], send_sem=fb_send.at[d], recv_sem=fb_recv.at[d],
            device_id={"x": xs[d]}, device_id_type=MESH)

    def ring_next(m):
        for way in range(2):
            row = ys[4 - m] if way == 0 else ys[4 + m]
            buf = (ryp, rym)[way]
            ring_copy(way, m - 1).wait_recv()
            part = slice(2 * way, 2 * way + 2) if m == 1 else slice(0, NX)
            cb[row, part] = cb[row, part] + buf[m - 1, part]
            ring_copy(way, m).start()

    def ring_last():
        ring_copy(0, 3).wait_recv()
        ring_copy(1, 3).wait_recv()
        cb[y] = cb[y] + ryp[3] + rym[3]
        for d in (2, 1, 3):
            fb_copy(d).start()

    def halves(r):
        return (0,) if r == MIXED else (0, 1)

    def o_copy(r):
        return pltpu.make_async_remote_copy(
            src_ref=sb.at[r], dst_ref=so.at[r], send_sem=o_send.at[r], recv_sem=o_recv.at[r],
            device_id={"c": other}, device_id_type=MESH)

    def first(r):
        rhs = jnp.concatenate([bb[0, pl.ds(NZL * block[r], NZL)].reshape(1536, 128), bb[1, pl.ds(NZL * block[r], NZL)].reshape(1536, 128)], axis=1)
        for cc in range(2):
            part = jnp.dot(a2[cc], rhs, preferred_element_type=jnp.float32).reshape(NX, NY, 8, 256)
            for h in halves(r):
                ca[r, h, :, :, cc] = part[:, :, :, h * 128:(h + 1) * 128]
            if r == MIXED:
                for xx in range(NX):
                    cb[:, xx, cc] = part[xx, :, :, 128:]
        if r == MIXED:
            ring_copy(0, 0).start()
            ring_copy(1, 0).start()
        for h in halves(r):
            for m in range(2):
                x_copy(r, h, 0, m).start()
                x_copy(r, h, 1, m).start()

    def second(r):
        for h in halves(r):
            x_copy(r, h, 0, 0).wait_recv()
            ca[r, h, xs[1], 0:4] = ca[r, h, xs[1], 0:4] + rxp[r, h, 0]
            x_copy(r, h, 0, 2).start()
            x_copy(r, h, 1, 0).wait_recv()
            ca[r, h, xs[3], 4:8] = ca[r, h, xs[3], 4:8] + rxm[r, h, 0]
            x_copy(r, h, 1, 2).start()

    def third(r):
        for h in halves(r):
            for m in range(1, 3):
                x_copy(r, h, 0, m).wait_recv()
                x_copy(r, h, 1, m).wait_recv()
            ca[r, h, x, 0:4] = ca[r, h, x, 0:4] + rxp[r, h, 2] + rxm[r, h, 1]
            ca[r, h, x, 4:8] = ca[r, h, x, 4:8] + rxp[r, h, 1] + rxm[r, h, 2]
            for d in (4, 3, 5, 2, 6, 1, 7):
                y_copy(r, h, d).start()

    def store(r, core, h, value):
        col = ((2 * core + h) * NZH + block[r]) * 128
        out_ref[:, pl.ds(pl.multiple_of(col, 128), 128)] = value

    def finish(r):
        for h in halves(r):
            for d in range(1, NY):
                y_copy(r, h, d).wait_recv()
        if r == MIXED:
            for d in range(1, NX):
                fb_copy(d).wait_recv()

        def rows(h, core):
            if h not in halves(r):
                total = cb[y, x, core]
                for d in range(1, NX):
                    total = total + fb[d, core]
                return total.astype(jnp.bfloat16)
            total = ca[r, h, x, y, core]
            for d in range(1, NY):
                total = total + fa[r, h, d, core]
            return total.astype(jnp.bfloat16)

        for h in range(2):
            sb[r, :, h * 128:(h + 1) * 128] = rows(h, other)
        o_copy(r).start()
        for h in range(2):
            store(r, c, h, rows(h, c))

    z_slots(0, 25)
    a_finish()
    z_slots(25, 26)
    sib_copy.wait_recv()
    first(0)
    z_slots(26, 28)
    first(1)
    z_slots(28, 30)
    second(0)
    z_slots(30, 32)
    first(2)
    second(1)
    third(0)
    z_far()
    first(3)
    ring_next(1)
    third(1)
    second(2)
    ring_next(2)
    second(3)
    finish(0)
    third(2)
    ring_next(3)
    finish(1)
    third(3)
    ring_last()
    finish(2)
    finish(3)

    for r in range(ROUNDS):
        o_copy(r).wait_recv()
        for h in range(2):
            store(r, other, h, so[r, :, h * 128:(h + 1) * 128])

    def a_left(i, _):
        a_copy(i).wait_send()
        return 0

    lax.fori_loop(1, NCHIP, a_left, 0)
    sib_copy.wait_send()

    for h in range(2):
        @pl.when(jnp.logical_not(b_stays(h)))
        def _():
            for part in range(2):
                b_copy(h, part).wait_send()

    for n in range(NSTEP):
        for way in range(2):
            if z_passes(n, way):
                z_copy(n, way).wait_send()
    for r in range(ROUNDS):
        for h in halves(r):
            for way in range(2):
                for m in range(3):
                    x_copy(r, h, way, m).wait_send()
            for d in range(1, NY):
                y_copy(r, h, d).wait_send()
        o_copy(r).wait_send()
    for way in range(2):
        for m in range(4):
            ring_copy(way, m).wait_send()
    for d in range(1, NX):
        fb_copy(d).wait_send()


def body(amplitudes, integrals, tile_mask, tile_size):
    dma = pltpu.SemaphoreType.DMA
    f32, bf16 = jnp.float32, jnp.bfloat16
    return pl.pallas_call(
        kernel,
        out_shape=jax.ShapeDtypeStruct((8, 2048), bf16),
        in_specs=[pl.BlockSpec(memory_space=pltpu.SMEM)] * 2 + [pl.BlockSpec(memory_space=pltpu.VMEM)] * 2,
        out_specs=pl.BlockSpec(memory_space=pltpu.VMEM),
        scratch_shapes=[
            pltpu.VMEM((NCHIP, 8, 1536), bf16),
            pltpu.VMEM((2, 256, 1536), bf16),
            pltpu.VMEM((2, NZ, 2, 192, 128), bf16),
            pltpu.VMEM((ROUNDS, 2, NX, NY, 2, 8, 128), f32),
            pltpu.VMEM((ROUNDS, 2, 3, 4, 2, 8, 128), f32),
            pltpu.VMEM((ROUNDS, 2, 3, 4, 2, 8, 128), f32),
            pltpu.VMEM((ROUNDS, 2, NY, 2, 8, 128), f32),
            pltpu.VMEM((NY, NX, 2, 8, 128), f32),
            pltpu.VMEM((4, NX, 2, 8, 128), f32),
            pltpu.VMEM((4, NX, 2, 8, 128), f32),
            pltpu.VMEM((NX, 2, 8, 128), f32),
            pltpu.VMEM((ROUNDS, 8, 256), bf16),
            pltpu.VMEM((ROUNDS, 8, 256), bf16),
            dma((NCHIP,)), dma((NCHIP,)), dma(()), dma(()), dma(()),
            dma((2, 2)), dma((2, 2)),
            dma((2, NSTEP)), dma((2, NSTEP + NPIECE)),
            dma((ROUNDS, 2, 2, 3)), dma((ROUNDS, 2, 2, 3)),
            dma((ROUNDS, 2, NY)), dma((ROUNDS, 2, NY)),
            dma((2, 4)), dma((2, 4)), dma((NX,)), dma((NX,)),
            dma((ROUNDS,)), dma((ROUNDS,)), pltpu.SemaphoreType.REGULAR,
            pltpu.SemaphoreType.REGULAR, pltpu.SemaphoreType.REGULAR,
        ],
        compiler_params=pltpu.CompilerParams(collective_id=0, has_side_effects=True),
    )(tile_mask, tile_size, amplitudes, integrals)


def solution(mesh):
    axes = ("x", "zh", "zl", "y", "c")
    fine = Mesh(mesh.devices.reshape(NX, NZH, NZL, NY, NC), axes)
    return jax.shard_map(
        body,
        mesh=fine,
        in_specs=(P(axes, None), P(("zl", "y", "c"), ("x", "zh")), P(axes, None), P()),
        out_specs=P(axes, None),
        check_vma=False,
    )
```
